256 devices in a mesh: dp: 16 (over z, y_hi), own: 16 (over y_lo, x, core).
Axes of the slice: x: 4, y: 4 (y_hi: 2, y_lo: 2; y = y_hi * 2 + y_lo), z: 8, core: 2. Of those that a mesh axis runs over, the one named last changes fastest.
Arguments:
- grad_parts: bfloat16 [16, 16, 1152, 1152], P('own', None, 'dp'), may hold values from -4.5 to 4.5
- owner_list: int32 [16], replicated, may hold values from 0 to 15, as said below
- left_stat: float32 [16, 3, 1152, 1152], P('own', None, 'dp'), may hold values from -3 to 3
- right_stat: float32 [16, 3, 1152, 1152], P('own', None, 'dp'), may hold values from -3 to 3
- second_moment: float32 [16, 3, 1152, 1152], P('own', None, 'dp'), may hold values from 0.1 to 10
- left_root: bfloat16 [16, 3, 1152, 1152], P('own', None, 'dp'), may hold values from -3 to 3
- right_root: bfloat16 [16, 3, 1152, 1152], P('own', None, 'dp'), may hold values from -3 to 3
- weights: bfloat16 [16, 3, 1152, 1152], P('own', None, 'dp'), may hold values from -6 to 6
Outputs:
- new_left: float32 [16, 3, 1152, 1152], P('own', None, 'dp')
- new_right: float32 [16, 3, 1152, 1152], P('own', None, 'dp')
- new_second: float32 [16, 3, 1152, 1152], P('own', None, 'dp')
- new_weights: bfloat16 [16, 1152, 1152], P(None, 'dp')
The draws below stay inside these ranges and needn't reach their ends.
Inputs may be any that keep to these rules, and one draw needn't show every extreme that they name: `owner_list`: no owner index is named by more than 3 blocks, and one is named by exactly 3.
All inputs are finite; a program needn't handle non-finite values.
Results may differ from the reference program's by a relative error of at most 0.02.
Values may be sent and summed in bfloat16 or wider, within the bound.
A program may use at most 128 MiB of HBM per device.

```python
import math
import jax
import jax.numpy as jnp
from jax import lax

P_SIZE = 1152
SLOTS = 3
UNITS = 16
N_OWN = 16


def symmetric_draw(key, diag_lo, diag_hi, spread):
    first, second = jax.random.split(key)
    noise = jnp.clip(jax.random.normal(first, (N_OWN, SLOTS, P_SIZE, P_SIZE), jnp.float32), -4.0, 4.0)
    mirrored = (noise + jnp.swapaxes(noise, 2, 3)) * (spread / math.sqrt(2.0 * P_SIZE))
    diagonal = jnp.exp(jax.random.uniform(second, (N_OWN, SLOTS, P_SIZE), jnp.float32, math.log(diag_lo), math.log(diag_hi)))
    on_diag = lax.broadcasted_iota(jnp.int32, (P_SIZE, P_SIZE), 0) == lax.broadcasted_iota(jnp.int32, (P_SIZE, P_SIZE), 1)
    return jnp.where(on_diag, diagonal[..., :, None], mirrored)


def draw_grad_parts(key, part):
    inner = jax.random.fold_in(key, 31)
    position = jnp.arange(P_SIZE, dtype=jnp.float32) / (P_SIZE - 1)
    shape = (N_OWN, UNITS, P_SIZE, P_SIZE)
    values = jnp.clip(jax.random.normal(inner, shape, jnp.float32), -6.0, 6.0)
    rising = 3.0 ** position
    return (values * (0.25 * rising)[None, None, :, None]).astype(jnp.bfloat16)


def draw_owner_list(key, part):
    base = jax.random.fold_in(key, 7)
    first, second, third = jax.random.split(base, 3)
    total = N_OWN * SLOTS
    if UNITS == SLOTS:
        busiest = jnp.int32(N_OWN - 1)
    else:
        busiest = jax.random.randint(first, (), 0, N_OWN).astype(jnp.int32)
    order = jax.random.permutation(second, jnp.arange(total, dtype=jnp.int32))
    holder = order // SLOTS
    priority = jnp.arange(total, dtype=jnp.int32) + jnp.where(holder == busiest, 2 * total, 0) - jnp.where(holder == N_OWN - 1, total, 0)
    ranked = order[jnp.argsort(priority, stable=True)]
    others = ranked[:UNITS - SLOTS] // SLOTS
    owners = jnp.concatenate([jnp.full((SLOTS,), busiest, jnp.int32), others.astype(jnp.int32)])
    return jax.random.permutation(third, owners).astype(jnp.int32)


def draw_left_stat(key, part):
    return symmetric_draw(jax.random.fold_in(key, 101), 1.0, 3.0, 0.3)


def draw_right_stat(key, part):
    return symmetric_draw(jax.random.fold_in(key, 102), 1.0, 3.0, 0.3)


def draw_left_root(key, part):
    return symmetric_draw(jax.random.fold_in(key, 103), 1.5, 3.0, 0.6).astype(jnp.bfloat16)


def draw_right_root(key, part):
    return symmetric_draw(jax.random.fold_in(key, 104), 1.5, 3.0, 0.6).astype(jnp.bfloat16)


def levels(rng, shape, cuts, smallest, largest):
    level = 1.0
    for dim, blocks in cuts:
        draws = jax.random.uniform(jax.random.fold_in(jax.random.fold_in(rng, 6), dim), (blocks,), jnp.float32, smallest / len(cuts), largest / len(cuts))
        level = level * jnp.repeat(jnp.exp(draws), shape[dim] // blocks).reshape((-1,) + (1,) * (len(shape) - 1 - dim))
    return level


def scatter_about(own_key, extent, deviation, bound, cuts=(), kind=jnp.bfloat16):
    gain = levels(own_key, extent, cuts, -0.22, 0.18) if cuts else 1.0
    array = jax.random.normal(own_key, extent, jnp.float32) * deviation * gain
    return jnp.minimum(jnp.maximum(array, -bound), bound).astype(kind)


def setup_inputs(seed: int = 0) -> dict:
    keys = jax.random.split(jax.random.key(seed), 9)
    grad_parts = draw_grad_parts(jax.random.fold_in(keys[8], 71), 0)
    owner_list = draw_owner_list(jax.random.fold_in(keys[8], 71), 0)
    left_stat = draw_left_stat(jax.random.fold_in(keys[8], 71), 0)
    right_stat = draw_right_stat(jax.random.fold_in(keys[8], 71), 0)
    second_moment = jnp.clip(jnp.exp(math.log(10.0) - 4.6051702 * jax.random.uniform(keys[4], (N_OWN, SLOTS, P_SIZE, P_SIZE), jnp.float32) ** levels(keys[4], (N_OWN, SLOTS, P_SIZE, P_SIZE), ((0, 16), (2, 16)), -0.2, 0.2)), 0.1, 10.0)
    left_root = draw_left_root(jax.random.fold_in(keys[8], 71), 0)
    right_root = draw_right_root(jax.random.fold_in(keys[8], 71), 0)
    weights = scatter_about(keys[7], (N_OWN, SLOTS, P_SIZE, P_SIZE), 1.0, 6.0, ((0, 16), (2, 16)))
    return {"grad_parts": grad_parts, "owner_list": owner_list, "left_stat": left_stat, "right_stat": right_stat, "second_moment": second_moment, "left_root": left_root, "right_root": right_root, "weights": weights}


def slot_tables(owner_list, owner_count, slot_count, unit_count):
    index = jnp.arange(unit_count, dtype=jnp.int32)
    earlier = (owner_list[:, None] == owner_list[None, :]) & (index[None, :] < index[:, None])
    rank = lax.optimization_barrier(jnp.sum(earlier.astype(jnp.int32), axis=1))
    slot_id = owner_list * slot_count + rank
    every_slot = jnp.arange(owner_count * slot_count, dtype=jnp.int32)
    match = (slot_id[None, :] == every_slot[:, None]).astype(jnp.int32)
    unit_of_slot = lax.optimization_barrier(jnp.sum(match * index[None, :], axis=1))
    filled = lax.optimization_barrier(jnp.sum(match, axis=1)) > 0
    return (slot_id, unit_of_slot, filled)

def reference(grad_parts, owner_list, left_stat, right_stat, second_moment, left_root, right_root, weights):
    slot_id, unit_of_slot, filled = slot_tables(owner_list, N_OWN, SLOTS, UNITS)

    def one_slot(position):
        owner = position // SLOTS
        place = position % SLOTS
        unit = unit_of_slot[position]
        parts = lax.dynamic_index_in_dim(grad_parts, unit, axis=1, keepdims=False)
        total = lax.optimization_barrier(jnp.sum(parts.astype(jnp.float32), axis=0))
        grad = jnp.where(filled[position], total, jnp.float32(0.0)).astype(jnp.bfloat16)
        left_gram = jnp.dot(grad, grad.T, preferred_element_type=jnp.float32)
        right_gram = jnp.dot(grad.T, grad, preferred_element_type=jnp.float32)
        new_left = 0.95 * left_stat[owner, place] + 0.05 / P_SIZE * left_gram
        new_right = 0.95 * right_stat[owner, place] + 0.05 / P_SIZE * right_gram
        gradient = grad.astype(jnp.float32)
        new_second = 0.95 * second_moment[owner, place] + 0.05 * gradient * gradient
        adam = gradient / (jnp.sqrt(new_second) + 1e-08)
        mixed = jnp.dot(left_root[owner, place], grad, preferred_element_type=jnp.float32).astype(jnp.bfloat16)
        precond = jnp.dot(mixed, right_root[owner, place], preferred_element_type=jnp.float32)
        graft = jnp.sqrt(jnp.sum(adam * adam) / (jnp.sum(precond * precond) + 1e-06))
        updated = (weights[owner, place].astype(jnp.float32) - 0.3 * graft * precond).astype(jnp.bfloat16)
        return (new_left, new_right, new_second, updated)
    new_left, new_right, new_second, updated = lax.map(one_slot, jnp.arange(N_OWN * SLOTS, dtype=jnp.int32))
    shape = (N_OWN, SLOTS, P_SIZE, P_SIZE)
    new_weights = jnp.take(updated, slot_id, axis=0)
    return (new_left.reshape(shape), new_right.reshape(shape), new_second.reshape(shape), new_weights)
```

```python
import functools

import jax
import jax.numpy as jnp
from jax import lax
from jax.experimental import pallas as pl
from jax.experimental.pallas import tpu as pltpu
from jax.sharding import PartitionSpec as P

MESH = pl.DeviceIdType.MESH
ROWS = 72
WIDTH = 1152
SLOTS = 3
ZS = 8


class Place:
    def __init__(self):
        self.dp = lax.axis_index("dp")
        self.own = lax.axis_index("own")
        self.z = self.dp // 2
        self.h = self.dp % 2
        self.c = self.own % 2
        self.right = self.at((self.dp + 2) % 16, self.own)
        self.left = self.at((self.dp + 14) % 16, self.own)
        self.pair = self.at(self.dp, self.own + 1 - 2 * self.c)
        self.fourth = self.at((self.dp + 16 + 2 * (1 - 2 * self.c)) % 16, self.own)
        self.swap = self.at(2 * self.z + self.c, self.own - self.c + self.h)
        self.swaps = self.c != self.h

    def at(self, dp, own):
        return {"dp": dp, "own": own}

    def block(self, step, core):
        return 2 * ((self.z + step + ZS) % ZS) + core


def rows(block):
    return pl.ds(pl.multiple_of(block * ROWS, 8), ROWS)


def remote(src, dst, send, recv, device):
    return pltpu.make_async_remote_copy(
        src_ref=src, dst_ref=dst, send_sem=send, recv_sem=recv, device_id=device, device_id_type=MESH
    )


def greet(place, devices):
    barrier = pltpu.get_barrier_semaphore()
    for device in devices:
        pl.semaphore_signal(barrier, inc=1, device_id=device, device_id_type=MESH)

    @pl.when(place.swaps)
    def _():
        pl.semaphore_signal(barrier, inc=1, device_id=place.swap, device_id_type=MESH)

    pl.semaphore_wait(barrier, len(devices) + place.swaps.astype(jnp.int32))


def exchange(place, moves, send, recv):
    @pl.when(place.swaps)
    def _():
        for i, (src, dst) in enumerate(moves):
            remote(src, dst, send.at[i], recv.at[i], place.swap).start()

    @pl.when(jnp.logical_not(place.swaps))
    def _():
        for i, (src, dst) in enumerate(moves):
            pltpu.make_async_copy(src, dst, recv.at[i]).start()


def exchange_wait(place, i, src, dst, send, recv):
    @pl.when(place.swaps)
    def _():
        remote(src, dst, send.at[i], recv.at[i], place.swap).wait()

    @pl.when(jnp.logical_not(place.swaps))
    def _():
        pltpu.make_async_copy(src, dst, recv.at[i]).wait()


class Ring:
    def __init__(self, place, full, sems):
        self.place, self.full = place, full
        self.ring_send, self.ring_recv, self.pair_send, self.pair_recv = sems
        self.started = []

    def send(self, slot, block, send, recv, device):
        window = self.full.at[slot, rows(block)]
        copy = remote(window, window, send, recv, device)
        copy.start()
        self.started.append(copy)

    def arrive(self, slot, block, send, recv):
        window = self.full.at[slot, rows(block)]
        remote(window, window, send, recv, self.place.pair).wait_recv()

    def ring(self, way, hop, slot, block, device):
        self.send(slot, block, self.ring_send.at[way, hop, slot], self.ring_recv.at[way, hop, slot], device)

    def hand(self, index, slot, block):
        self.send(slot, block, self.pair_send.at[index, slot], self.pair_recv.at[index, slot], self.place.pair)

    def begin(self, slot):
        p = self.place
        own = p.block(0, p.c)
        self.ring(0, 0, slot, own, p.right)
        self.ring(1, 0, slot, own, p.left)
        self.hand(0, slot, own)

    def hop(self, k, slot):
        p = self.place
        if k < 4:
            from_left, from_right = p.block(-k, p.c), p.block(k, p.c)
            self.arrive(slot, from_left, self.ring_send.at[0, k - 1, slot], self.ring_recv.at[0, k - 1, slot])
            if k < 3:
                self.ring(0, k, slot, from_left, p.right)
            self.hand(k, slot, from_left)
            self.arrive(slot, from_right, self.ring_send.at[1, k - 1, slot], self.ring_recv.at[1, k - 1, slot])
            if k < 3:
                self.ring(1, k, slot, from_right, p.left)
            else:
                last = p.block(-3 * (1 - 2 * p.c), p.c)
                self.ring(0, 3, slot, last, p.fourth)
            self.hand(3 + k, slot, from_right)
        else:
            far = p.block(4, p.c)
            self.arrive(slot, far, self.ring_send.at[0, 3, slot], self.ring_recv.at[0, 3, slot])
            self.hand(7, slot, far)

    def handed(self, slot):
        p = self.place
        steps = [0, -1, -2, -3, 1, 2, 3, 4]
        for index, step in enumerate(steps):
            self.arrive(slot, p.block(step, 1 - p.c), self.pair_send.at[index, slot], self.pair_recv.at[index, slot])

    def finish(self):
        for copy in self.started:
            copy.wait_send()


RING_SEMS = [
    pltpu.SemaphoreType.DMA((2, 4, SLOTS)),
    pltpu.SemaphoreType.DMA((2, 4, SLOTS)),
    pltpu.SemaphoreType.DMA((8, SLOTS)),
    pltpu.SemaphoreType.DMA((8, SLOTS)),
]


def roots_kernel(left_ref, right_ref, left_out, full_out, swap_send, swap_recv, *sems):
    place = Place()
    greet(place, [place.right, place.left, place.pair])
    moves = [(right_ref.at[s], full_out.at[s, rows(place.dp)]) for s in range(SLOTS)]
    moves += [(left_ref.at[s], left_out.at[s]) for s in range(SLOTS)]
    exchange(place, moves, swap_send, swap_recv)
    ring = Ring(place, full_out, sems)
    for slot in range(SLOTS):
        src, _ = moves[slot]
        exchange_wait(place, slot, src, full_out.at[slot, rows(place.block(0, place.c))], swap_send, swap_recv)
        ring.begin(slot)
    for k in range(1, 5):
        for slot in range(SLOTS):
            ring.hop(k, slot)
    for slot in range(SLOTS):
        ring.handed(slot)
        src, dst = moves[SLOTS + slot]
        exchange_wait(place, SLOTS + slot, src, dst, swap_send, swap_recv)
    ring.finish()


def gather_roots(left_root, right_root):
    anywhere = pl.BlockSpec(memory_space=pl.ANY)
    return pl.pallas_call(
        roots_kernel,
        out_shape=(
            jax.ShapeDtypeStruct((SLOTS, ROWS, WIDTH), jnp.bfloat16),
            jax.ShapeDtypeStruct((SLOTS, WIDTH, WIDTH), jnp.bfloat16),
        ),
        in_specs=[anywhere, anywhere],
        out_specs=(anywhere, anywhere),
        scratch_shapes=[
            pltpu.SemaphoreType.DMA((2 * SLOTS,)),
            pltpu.SemaphoreType.DMA((2 * SLOTS,)),
            *RING_SEMS,
        ],
        compiler_params=pltpu.CompilerParams(collective_id=0, has_side_effects=True),
        cost_estimate=pl.CostEstimate(flops=0, bytes_accessed=100_000_000, transcendentals=0),
        name="gather_roots",
    )(left_root, right_root)


NT = (((1,), (1,)), ((), ()))


def main_kernel(
    grad_ref, left_ref, right_ref, weight_ref, adam_ref,
    gram_left_ref, gram_right_ref, new_ref, full_hbm,
    full, right_full, results, returned, sums, totals,
    swap_send, swap_recv, back_send, back_recv, local_sem, sum_send, sum_recv, *sems
):
    place = Place()
    peers = [place.at((place.dp + d) % 16, place.own) for d in range(1, 16)]
    greet(place, [place.pair, *peers])
    load_right = pltpu.make_async_copy(right_ref, right_full, local_sem.at[0])
    load_right.start()
    moves = [(grad_ref.at[s], full_hbm.at[s, rows(place.dp)]) for s in range(SLOTS)]
    exchange(place, moves, swap_send, swap_recv)
    ring = Ring(place, full_hbm, sems)
    work = place.block(0, place.c)
    for slot in range(SLOTS):
        src, _ = moves[slot]
        exchange_wait(place, slot, src, full_hbm.at[slot, rows(work)], swap_send, swap_recv)
        ring.begin(slot)
    for k in range(1, 5):
        for slot in range(SLOTS):
            ring.hop(k, slot)
    for slot in range(SLOTS):
        ring.handed(slot)
        pltpu.make_async_copy(full_hbm.at[slot], full.at[slot], local_sem.at[1 + slot]).start()
    ring.finish()
    load_right.wait()
    lane = lax.broadcasted_iota(jnp.int32, (ROWS, WIDTH), 1)
    row = lax.broadcasted_iota(jnp.int32, (ROWS, WIDTH), 0)
    pick = jnp.where(lane == row + work * ROWS, 1.0, 0.0).astype(jnp.bfloat16)
    for slot in range(SLOTS):
        pltpu.make_async_copy(full_hbm.at[slot], full.at[slot], local_sem.at[1 + slot]).wait()

    def compute(slot, carry):
        grad = full[slot]
        mine = jnp.dot(pick, grad, preferred_element_type=jnp.float32).astype(jnp.bfloat16)
        results[slot, 0] = lax.dot_general(mine, grad, NT, preferred_element_type=jnp.float32).astype(jnp.bfloat16)
        columns = lax.dot_general(pick, grad, NT, preferred_element_type=jnp.float32).astype(jnp.bfloat16)
        results[slot, 1] = jnp.dot(columns, grad, preferred_element_type=jnp.float32).astype(jnp.bfloat16)
        mixed = jnp.dot(left_ref[slot], grad, preferred_element_type=jnp.float32).astype(jnp.bfloat16)
        precond = jnp.dot(mixed, right_full[slot], preferred_element_type=jnp.float32)
        results[slot, 2] = precond.astype(jnp.bfloat16)
        return carry

    lax.fori_loop(0, SLOTS, compute, 0)
    back = [(results.at[s, i], returned.at[s, i]) for s in range(SLOTS) for i in (2, 0, 1)]
    exchange(place, back, back_send, back_recv)
    for i, (src, dst) in enumerate(back):
        exchange_wait(place, i, src, dst, back_send, back_recv)

    spread = jnp.zeros((8, 128), jnp.float32)
    index = lax.broadcasted_iota(jnp.int32, (8, 128), 0)
    for slot in range(SLOTS):
        precond = returned[slot, 2].astype(jnp.float32)
        spread = spread + jnp.where(index == slot, jnp.sum(precond * precond), 0.0)
    sums[...] = spread + adam_ref[...]
    copies = []
    for d, peer in enumerate(peers):
        copies.append(remote(sums, totals.at[d], sum_send.at[d], sum_recv.at[d], peer))
        copies[-1].start()
    gram_left_ref[...] = returned[:, 0]
    gram_right_ref[...] = returned[:, 1]
    total = sums[...]
    for d, copy in enumerate(copies):
        copy.wait()
        total = total + totals[d]
    for slot in range(SLOTS):
        pre_total, adam_total = total[slot : slot + 1, 0:1], total[slot + 3 : slot + 4, 0:1]
        graft = jnp.sqrt(adam_total / (pre_total + 1e-06))
        precond = returned[slot, 2].astype(jnp.float32)
        new_ref[slot] = (weight_ref[slot].astype(jnp.float32) - 0.3 * graft * precond).astype(jnp.bfloat16)


def precondition(grads, left_rows, right_full, weights, adam):
    anywhere = pl.BlockSpec(memory_space=pl.ANY)
    vmem = pl.BlockSpec(memory_space=pltpu.VMEM)
    small = jax.ShapeDtypeStruct((SLOTS, ROWS, WIDTH), jnp.bfloat16)
    return pl.pallas_call(
        main_kernel,
        out_shape=(small, small, small, jax.ShapeDtypeStruct((SLOTS, WIDTH, WIDTH), jnp.bfloat16)),
        in_specs=[anywhere, vmem, anywhere, vmem, vmem],
        out_specs=(vmem, vmem, vmem, anywhere),
        scratch_shapes=[
            pltpu.VMEM((SLOTS, WIDTH, WIDTH), jnp.bfloat16),
            pltpu.VMEM((SLOTS, WIDTH, WIDTH), jnp.bfloat16),
            pltpu.VMEM((SLOTS, 3, ROWS, WIDTH), jnp.bfloat16),
            pltpu.VMEM((SLOTS, 3, ROWS, WIDTH), jnp.bfloat16),
            pltpu.VMEM((8, 128), jnp.float32),
            pltpu.VMEM((15, 8, 128), jnp.float32),
            pltpu.SemaphoreType.DMA((SLOTS,)),
            pltpu.SemaphoreType.DMA((SLOTS,)),
            pltpu.SemaphoreType.DMA((3 * SLOTS,)),
            pltpu.SemaphoreType.DMA((3 * SLOTS,)),
            pltpu.SemaphoreType.DMA((1 + SLOTS,)),
            pltpu.SemaphoreType.DMA((15,)),
            pltpu.SemaphoreType.DMA((15,)),
            *RING_SEMS,
        ],
        compiler_params=pltpu.CompilerParams(
            collective_id=1, has_side_effects=True, vmem_limit_bytes=60 * 1024 * 1024
        ),
        name="precondition",
    )(grads, left_rows, right_full, weights, adam)


def slot_tables(owner_list, owner_count, slot_count, unit_count):
    index = jnp.arange(unit_count, dtype=jnp.int32)
    earlier = (owner_list[:, None] == owner_list[None, :]) & (index[None, :] < index[:, None])
    rank = jnp.sum(earlier.astype(jnp.int32), axis=1)
    slot_id = owner_list * slot_count + rank
    every_slot = jnp.arange(owner_count * slot_count, dtype=jnp.int32)
    match = (slot_id[None, :] == every_slot[:, None]).astype(jnp.int32)
    unit_of_slot = jnp.sum(match * index[None, :], axis=1)
    filled = jnp.sum(match, axis=1) > 0
    return (slot_id, unit_of_slot, filled)


def local(
    grad_parts, owner_list, left_stat, right_stat, second_moment, left_root, right_root, weights
):
    owner_count = lax.axis_size("own")
    unit_count = owner_list.shape[0]
    slot_id, unit_of_slot, filled = slot_tables(owner_list, owner_count, SLOTS, unit_count)
    me = lax.axis_index("own")
    units = lax.dynamic_slice_in_dim(unit_of_slot, me * SLOTS, SLOTS)
    mine = lax.dynamic_slice_in_dim(filled, me * SLOTS, SLOTS)

    left_rows, right_full = gather_roots(left_root[0], right_root[0])
    summed = lax.psum(grad_parts[0], "own")
    grads = jnp.where(mine[:, None, None], jnp.take(summed, units, axis=0), jnp.bfloat16(0.0))

    gradient = grads.astype(jnp.float32)
    new_second = 0.95 * second_moment[0] + 0.05 * gradient * gradient
    adam = gradient / (jnp.sqrt(new_second) + 1e-08)
    adam_sums = jnp.sum(adam * adam, axis=(1, 2))
    adam_tile = jnp.broadcast_to(jnp.pad(adam_sums, (3, 2))[:, None], (8, 128))

    gram_left, gram_right, new_rows, _ = precondition(grads, left_rows, right_full, weights[0], adam_tile)
    scale = 0.05 / WIDTH
    new_left = 0.95 * left_stat + scale * gram_left.astype(jnp.float32)[None]
    new_right = 0.95 * right_stat + scale * gram_right.astype(jnp.float32)[None]
    every_rows = lax.all_gather(new_rows, "own", axis=0, tiled=True)
    new_weights = jnp.take(every_rows, slot_id, axis=0)
    return (new_left, new_right, new_second[None], new_weights)


def solution(mesh):
    placed = P("own", None, "dp", None)
    in_specs = (placed, P(), placed, placed, placed, placed, placed, placed)
    out_specs = (placed, placed, placed, P(None, "dp", None))
    return jax.shard_map(local, mesh=mesh, in_specs=in_specs, out_specs=out_specs, check_vma=False)
```

```python
import functools

import jax
import jax.numpy as jnp
from jax import lax
from jax.experimental import pallas as pl
from jax.experimental.pallas import tpu as pltpu
from jax.sharding import PartitionSpec as P

MESH = pl.DeviceIdType.MESH
ROWS = 72
WIDTH = 1152
SLOTS = 3
ZS = 8


class Place:
    def __init__(self):
        self.dp = lax.axis_index("dp")
        self.own = lax.axis_index("own")
        self.z = self.dp // 2
        self.h = self.dp % 2
        self.c = self.own % 2
        self.right = self.at((self.dp + 2) % 16, self.own)
        self.left = self.at((self.dp + 14) % 16, self.own)
        self.pair = self.at(self.dp, self.own + 1 - 2 * self.c)
        self.fourth = self.at((self.dp + 16 + 2 * (1 - 2 * self.c)) % 16, self.own)
        self.swap = self.at(2 * self.z + self.c, self.own - self.c + self.h)
        self.swaps = self.c != self.h
        self.x = self.own // 2 % 4
        self.y = self.own // 8
        self.x_right = self.at(self.dp, self.chip(0, 1))
        self.x_left = self.at(self.dp, self.chip(0, -1))
        self.y_other = self.at(self.dp, self.chip(1, 0))
        self.way = 1 - 2 * self.c
        self.x_ahead = self.at(self.dp, self.chip(0, self.way))
        self.x_behind = self.at(self.dp, self.chip(0, -self.way))

    def at(self, dp, own):
        return {"dp": dp, "own": own}

    def chip(self, dy, dx):
        return 2 * (4 * ((self.y + dy) % 2) + (self.x + dx + 4) % 4) + self.c

    def block(self, step, core):
        return 2 * ((self.z + step + ZS) % ZS) + core


def rows(block):
    return pl.ds(pl.multiple_of(block * ROWS, 8), ROWS)


def remote(src, dst, send, recv, device):
    return pltpu.make_async_remote_copy(
        src_ref=src, dst_ref=dst, send_sem=send, recv_sem=recv, device_id=device, device_id_type=MESH
    )


def greet(place, devices):
    barrier = pltpu.get_barrier_semaphore()
    for device in devices:
        pl.semaphore_signal(barrier, inc=1, device_id=device, device_id_type=MESH)

    @pl.when(place.swaps)
    def _():
        pl.semaphore_signal(barrier, inc=1, device_id=place.swap, device_id_type=MESH)

    pl.semaphore_wait(barrier, len(devices) + place.swaps.astype(jnp.int32))


def exchange(place, moves, send, recv):
    @pl.when(place.swaps)
    def _():
        for i, (src, dst) in enumerate(moves):
            remote(src, dst, send.at[i], recv.at[i], place.swap).start()

    @pl.when(jnp.logical_not(place.swaps))
    def _():
        for i, (src, dst) in enumerate(moves):
            pltpu.make_async_copy(src, dst, recv.at[i]).start()


def exchange_wait(place, i, src, dst, send, recv):
    @pl.when(place.swaps)
    def _():
        remote(src, dst, send.at[i], recv.at[i], place.swap).wait()

    @pl.when(jnp.logical_not(place.swaps))
    def _():
        pltpu.make_async_copy(src, dst, recv.at[i]).wait()


class Ring:
    def __init__(self, place, full, sems):
        self.place, self.full = place, full
        self.ring_send, self.ring_recv, self.pair_send, self.pair_recv = sems
        self.started = []

    def send(self, slot, block, send, recv, device):
        window = self.full.at[slot, rows(block)]
        copy = remote(window, window, send, recv, device)
        copy.start()
        self.started.append(copy)

    def arrive(self, slot, block, send, recv):
        window = self.full.at[slot, rows(block)]
        remote(window, window, send, recv, self.place.pair).wait_recv()

    def ring(self, way, hop, slot, block, device):
        self.send(slot, block, self.ring_send.at[way, hop, slot], self.ring_recv.at[way, hop, slot], device)

    def hand(self, index, slot, block):
        self.send(slot, block, self.pair_send.at[index, slot], self.pair_recv.at[index, slot], self.place.pair)

    def begin(self, slot):
        p = self.place
        own = p.block(0, p.c)
        self.ring(0, 0, slot, own, p.right)
        self.ring(1, 0, slot, own, p.left)
        self.hand(0, slot, own)

    def hop(self, k, slot):
        p = self.place
        if k < 4:
            from_left, from_right = p.block(-k, p.c), p.block(k, p.c)
            self.arrive(slot, from_left, self.ring_send.at[0, k - 1, slot], self.ring_recv.at[0, k - 1, slot])
            if k < 3:
                self.ring(0, k, slot, from_left, p.right)
            self.hand(k, slot, from_left)
            self.arrive(slot, from_right, self.ring_send.at[1, k - 1, slot], self.ring_recv.at[1, k - 1, slot])
            if k < 3:
                self.ring(1, k, slot, from_right, p.left)
            else:
                last = p.block(-3 * (1 - 2 * p.c), p.c)
                self.ring(0, 3, slot, last, p.fourth)
            self.hand(3 + k, slot, from_right)
        else:
            far = p.block(4, p.c)
            self.arrive(slot, far, self.ring_send.at[0, 3, slot], self.ring_recv.at[0, 3, slot])
            self.hand(7, slot, far)

    def handed(self, slot):
        p = self.place
        steps = [0, -1, -2, -3, 1, 2, 3, 4]
        for index, step in enumerate(steps):
            self.arrive(slot, p.block(step, 1 - p.c), self.pair_send.at[index, slot], self.pair_recv.at[index, slot])

    def finish(self):
        for copy in self.started:
            copy.wait_send()


RING_SEMS = [
    pltpu.SemaphoreType.DMA((2, 4, SLOTS)),
    pltpu.SemaphoreType.DMA((2, 4, SLOTS)),
    pltpu.SemaphoreType.DMA((8, SLOTS)),
    pltpu.SemaphoreType.DMA((8, SLOTS)),
]


class OwnGather:
    PLACES = [(dy, dx) for dy in (0, 1) for dx in (0, 1, -1, 2)]

    def __init__(self, place, window, sems, y_first):
        self.place, self.window, self.y_first = place, window, y_first
        self.send_sem, self.recv_sem, self.pair_send, self.pair_recv = sems
        self.started = []

    def index(self, dy, dx):
        return self.PLACES.index((dy, dx))

    def put(self, own, dy, dx, device, source=None):
        i = self.index(dy, dx)
        window = self.window(own)
        copy = remote(window if source is None else source, window, self.send_sem.at[i], self.recv_sem.at[i], device)
        copy.start()
        self.started.append(copy)

    def hand(self, dy, dx, source=None):
        i = self.index(dy, dx)
        window = self.window(self.place.chip(dy, dx))
        copy = remote(
            window if source is None else source, window, self.pair_send.at[i], self.pair_recv.at[i], self.place.pair
        )
        copy.start()
        self.started.append(copy)

    def arrive(self, dy, dx):
        i = self.index(dy, dx)
        window = self.window(self.place.chip(dy, dx))
        remote(window, window, self.send_sem.at[i], self.recv_sem.at[i], self.place.pair).wait_recv()

    def begin(self, source):
        p = self.place
        own = p.own
        if self.y_first:
            self.put(own, 1, 0, p.y_other, source)
        self.put(own, 0, -1, p.x_right, source)
        self.put(own, 0, 1, p.x_left, source)
        if not self.y_first:
            self.put(own, 1, 0, p.y_other, source)
        self.hand(0, 0, source)

    def across(self):
        p = self.place
        self.arrive(1, 0)
        if self.y_first:
            self.put(p.chip(1, 0), 1, -1, p.x_right)
            self.put(p.chip(1, 0), 1, 1, p.x_left)
        self.hand(1, 0)

    def near(self, dy):
        p = self.place
        self.arrive(dy, -1)
        self.arrive(dy, 1)
        if self.y_first or dy == 0:
            self.put(p.chip(dy, -p.way), dy, 2, p.x_ahead)
        if dy == 0 and not self.y_first:
            self.put(p.chip(0, -1), 1, -1, p.y_other)
            self.put(p.chip(0, 1), 1, 1, p.y_other)
        self.hand(dy, -1)
        self.hand(dy, 1)

    def far(self, dy):
        self.arrive(dy, 2)
        if dy == 0 and not self.y_first:
            self.put(self.place.chip(0, 2), 1, 2, self.place.y_other)
        self.hand(dy, 2)

    def handed(self):
        p = self.place
        for dy, dx in self.PLACES:
            i = self.index(dy, dx)
            window = self.window(p.chip(dy, dx) + 1 - 2 * p.c)
            remote(window, window, self.pair_send.at[i], self.pair_recv.at[i], p.pair).wait_recv()

    def finish(self):
        for copy in self.started:
            copy.wait_send()


OWN_SEMS = [pltpu.SemaphoreType.DMA((8,))] * 4


class OwnSum:
    def __init__(self, place, parts, buffers, sems):
        self.place, self.parts = place, parts
        self.mine, self.inbox, self.chip_sum, self.relay, self.mail, self.total = buffers
        self.load_sem, self.core_send, self.core_recv, self.mail_send, self.mail_recv = sems
        self.started = []

    def unit(self, ky, dx):
        return 4 * ky + (self.place.x + dx + 4) % 4

    def begin(self):
        p = self.place
        for dx in (2, p.way, -p.way, 0):
            for ky in range(2):
                k = self.unit(ky, dx)
                copy = remote(self.parts.at[k, 1 - p.c], self.inbox.at[k], self.core_send.at[k], self.core_recv.at[k], p.pair)
                copy.start()
                self.started.append(copy)
        for dx in (2, -p.way, p.way, 0):
            for ky in range(2):
                k = self.unit(ky, dx)
                pltpu.make_async_copy(self.parts.at[k, p.c], self.mine.at[k], self.load_sem.at[k]).start()

    def of_chip(self, ky, dx):
        p = self.place
        k = self.unit(ky, dx)
        remote(self.parts.at[k, p.c], self.inbox.at[k], self.core_send.at[k], self.core_recv.at[k], p.pair).wait_recv()
        pltpu.make_async_copy(self.parts.at[k, p.c], self.mine.at[k], self.load_sem.at[k]).wait()
        return self.mine[k].astype(jnp.float32) + self.inbox[k].astype(jnp.float32)

    def post(self, source, index, device):
        copy = remote(source, self.mail.at[index], self.mail_send.at[index], self.mail_recv.at[index], device)
        copy.start()
        self.started.append(copy)

    def receive(self, index):
        window = self.mail.at[index]
        remote(window, window, self.mail_send.at[index], self.mail_recv.at[index], self.place.pair).wait_recv()
        return self.mail[index].astype(jnp.float32)

    def out_far(self, ky):
        self.chip_sum[ky] = self.of_chip(ky, 2).astype(jnp.bfloat16)
        self.post(self.chip_sum.at[ky], ky, self.place.x_ahead)

    def out_near(self, ky):
        self.chip_sum[2 + ky] = self.of_chip(ky, -self.place.way).astype(jnp.bfloat16)
        self.post(self.chip_sum.at[2 + ky], 2 + ky, self.place.x_behind)

    def on(self, ky):
        own = self.of_chip(ky, self.place.way)
        self.relay[ky] = (self.receive(ky) + own).astype(jnp.bfloat16)
        self.post(self.relay.at[ky], 4 + ky, self.place.x_ahead)

    def cross(self):
        p = self.place
        ky = 1 - p.y
        own = self.of_chip(ky, 0)
        self.relay[2] = (own + self.receive(2 + ky) + self.receive(4 + ky)).astype(jnp.bfloat16)
        self.post(self.relay.at[2], 6, p.y_other)

    def end(self):
        p = self.place
        own = self.of_chip(p.y, 0) + self.receive(2 + p.y) + self.receive(4 + p.y)
        self.total[...] = (own + self.receive(6)).astype(jnp.bfloat16)

    def finish(self):
        for copy in self.started:
            copy.wait_send()


def block_buffer(count):
    return pltpu.VMEM((count, ROWS, WIDTH), jnp.bfloat16)


SUM_SCRATCH = [
    block_buffer(8),
    block_buffer(8),
    block_buffer(4),
    block_buffer(3),
    block_buffer(7),
    pltpu.VMEM((ROWS, WIDTH), jnp.bfloat16),
    pltpu.SemaphoreType.DMA((8,)),
    pltpu.SemaphoreType.DMA((8,)),
    pltpu.SemaphoreType.DMA((8,)),
    pltpu.SemaphoreType.DMA((7,)),
    pltpu.SemaphoreType.DMA((7,)),
]


def roots_kernel(parts_ref, left_ref, right_ref, left_out, full_out, sum_out, swap_send, swap_recv, own_sem, *rest):
    ring_sems, gather_sems, sum_scratch = rest[:4], rest[4:8], rest[8:]
    place = Place()
    greet(place, [place.right, place.left, place.pair, place.x_right, place.x_left, place.y_other])
    total = OwnSum(place, parts_ref, sum_scratch[:6], sum_scratch[6:])
    total.begin()
    moves = [(right_ref.at[s], full_out.at[s, rows(place.dp)]) for s in range(SLOTS)]
    moves += [(left_ref.at[s], left_out.at[s]) for s in range(SLOTS)]
    exchange(place, moves, swap_send, swap_recv)
    ring = Ring(place, full_out, ring_sems)

    def begin(slot):
        src, _ = moves[slot]
        exchange_wait(place, slot, src, full_out.at[slot, rows(place.block(0, place.c))], swap_send, swap_recv)
        ring.begin(slot)

    every = OwnGather(place, lambda own: sum_out.at[own], gather_sems, True)
    total.out_far(0)
    total.out_far(1)
    begin(0)
    total.out_near(0)
    total.out_near(1)
    begin(1)
    total.on(0)
    begin(2)
    ring.hop(1, 0)
    total.on(1)
    ring.hop(1, 1)
    total.cross()
    ring.hop(1, 2)
    total.end()
    every.begin(total.total)
    keep = pltpu.make_async_copy(total.total, sum_out.at[place.own], own_sem)
    keep.start()
    ring.hop(2, 0)
    every.across()
    ring.hop(2, 1)
    every.near(0)
    ring.hop(2, 2)
    every.near(1)
    ring.hop(3, 0)
    every.far(0)
    ring.hop(3, 1)
    every.far(1)
    ring.hop(3, 2)
    for slot in range(SLOTS):
        ring.hop(4, slot)
    every.handed()
    for slot in range(SLOTS):
        ring.handed(slot)
        src, dst = moves[SLOTS + slot]
        exchange_wait(place, SLOTS + slot, src, dst, swap_send, swap_recv)
    keep.wait()
    for part in (total, every, ring):
        part.finish()


def gather_roots(parts, left_root, right_root):
    anywhere = pl.BlockSpec(memory_space=pl.ANY)
    return pl.pallas_call(
        roots_kernel,
        out_shape=(
            jax.ShapeDtypeStruct((SLOTS, ROWS, WIDTH), jnp.bfloat16),
            jax.ShapeDtypeStruct((SLOTS, WIDTH, WIDTH), jnp.bfloat16),
            jax.ShapeDtypeStruct((16, ROWS, WIDTH), jnp.bfloat16),
        ),
        in_specs=[anywhere] * 3,
        out_specs=(anywhere,) * 3,
        scratch_shapes=[
            pltpu.SemaphoreType.DMA((2 * SLOTS,)),
            pltpu.SemaphoreType.DMA((2 * SLOTS,)),
            pltpu.SemaphoreType.DMA,
            *RING_SEMS,
            *OWN_SEMS,
            *SUM_SCRATCH,
        ],
        compiler_params=pltpu.CompilerParams(collective_id=0, has_side_effects=True),
        name="gather_roots",
    )(parts, left_root, right_root)


NT = (((1,), (1,)), ((), ()))


def main_kernel(
    slot_ref, grad_ref, left_ref, right_ref, weight_ref, adam_ref,
    gram_left_ref, gram_right_ref, new_ref, full_hbm,
    full, right_full, results, returned, updated, every, sums, totals,
    swap_send, swap_recv, back_send, back_recv, local_sem, sum_send, sum_recv, *sems
):
    place = Place()
    peers = [place.at((place.dp + d) % 16, place.own) for d in range(1, 16)]
    greet(place, [place.pair, place.x_right, place.x_left, place.y_other, *peers])
    moves = [(grad_ref.at[s], full_hbm.at[s, rows(place.dp)]) for s in range(SLOTS)]
    exchange(place, moves, swap_send, swap_recv)
    load_right = pltpu.make_async_copy(right_ref, right_full, local_sem.at[0])
    load_right.start()
    ring = Ring(place, full_hbm, sems[:4])
    work = place.block(0, place.c)
    lane = lax.broadcasted_iota(jnp.int32, (ROWS, WIDTH), 1)
    row = lax.broadcasted_iota(jnp.int32, (ROWS, WIDTH), 0)
    pick = jnp.where(lane == row + work * ROWS, 1.0, 0.0).astype(jnp.bfloat16)

    def begin(slot):
        src, _ = moves[slot]
        exchange_wait(place, slot, src, full_hbm.at[slot, rows(work)], swap_send, swap_recv)
        ring.begin(slot)

    def load(slot):
        return pltpu.make_async_copy(full_hbm.at[slot], full.at[slot], local_sem.at[1 + slot])

    back = {}
    for s in range(SLOTS):
        back[s, 0] = (results.at[s, 0], gram_left_ref.at[s])
        back[s, 1] = (results.at[s, 1], gram_right_ref.at[s])
        back[s, 2] = (results.at[s, 2], returned.at[s])

    def give(slot, which):
        i = 3 * slot + which
        exchange(place, [back[slot, which]], back_send.at[pl.ds(i, 1)], back_recv.at[pl.ds(i, 1)])

    def given(slot, which):
        exchange_wait(place, 3 * slot + which, *back[slot, which], back_send, back_recv)

    def solve(slot):
        mixed = jnp.dot(left_ref[slot], full[slot], preferred_element_type=jnp.float32).astype(jnp.bfloat16)
        precond = jnp.dot(mixed, right_full[slot], preferred_element_type=jnp.float32)
        results[slot, 2] = precond.astype(jnp.bfloat16)

    def grams(slot):
        grad = full[slot]
        mine = jnp.dot(pick, grad, preferred_element_type=jnp.float32).astype(jnp.bfloat16)
        results[slot, 0] = lax.dot_general(mine, grad, NT, preferred_element_type=jnp.float32).astype(jnp.bfloat16)
        columns = lax.dot_general(pick, grad, NT, preferred_element_type=jnp.float32).astype(jnp.bfloat16)
        results[slot, 1] = jnp.dot(columns, grad, preferred_element_type=jnp.float32).astype(jnp.bfloat16)

    begin(0)
    begin(1)
    ring.hop(1, 0)
    begin(2)
    ring.hop(1, 1)
    ring.hop(2, 0)
    ring.hop(1, 2)
    ring.hop(2, 1)
    ring.hop(3, 0)
    ring.hop(2, 2)
    ring.hop(3, 1)
    ring.hop(4, 0)
    ring.handed(0)
    load(0).start()
    load_right.wait()
    load(0).wait()
    solve(0)
    give(0, 2)
    ring.hop(3, 2)
    ring.hop(4, 1)
    grams(0)
    give(0, 0)
    give(0, 1)
    ring.hop(4, 2)
    ring.handed(1)
    load(1).start()
    ring.handed(2)
    load(2).start()
    load(1).wait()
    solve(1)
    give(1, 2)
    load(2).wait()
    solve(2)
    give(2, 2)
    grams(1)
    give(1, 0)
    give(1, 1)

    spread = adam_ref[...]
    index = lax.broadcasted_iota(jnp.int32, (8, 128), 0)
    for slot in range(SLOTS):
        given(slot, 2)
        precond = returned[slot].astype(jnp.float32)
        spread = spread + jnp.where(index == slot, jnp.sum(precond * precond), 0.0)
    sums[...] = spread
    copies = []
    for d, peer in enumerate(peers):
        copies.append(remote(sums, totals.at[d], sum_send.at[d], sum_recv.at[d], peer))
        copies[-1].start()
    grams(2)
    give(2, 0)
    give(2, 1)
    total = sums[...]
    for d, copy in enumerate(copies):
        copy.wait_recv()
        total = total + totals[d]

    gathers = []
    for slot in range(SLOTS):
        window = functools.partial(lambda slot, own: every.at[SLOTS * own + slot], slot)
        own_sems = [sem.at[slot] for sem in sems[4:8]]
        gathers.append(OwnGather(place, window, own_sems, slot > 0))
    for slot in range(SLOTS):
        pre_total, adam_total = total[slot : slot + 1, 0:1], total[slot + 3 : slot + 4, 0:1]
        graft = jnp.sqrt(adam_total / (pre_total + 1e-06))
        precond = returned[slot].astype(jnp.float32)
        updated[slot] = (weight_ref[slot].astype(jnp.float32) - 0.3 * graft * precond).astype(jnp.bfloat16)
        gathers[slot].begin(updated.at[slot])
        pltpu.make_async_copy(updated.at[slot], every.at[SLOTS * place.own + slot], local_sem.at[4 + slot]).start()
    gathers[0].near(0)
    gathers[1].across()
    gathers[2].across()
    gathers[1].near(0)
    gathers[2].near(0)
    gathers[0].across()
    gathers[0].far(0)
    gathers[1].near(1)
    gathers[2].near(1)
    gathers[0].near(1)
    gathers[1].far(0)
    gathers[2].far(0)
    gathers[0].far(1)
    gathers[1].far(1)
    gathers[2].far(1)
    for slot in range(SLOTS):
        gathers[slot].handed()
        pltpu.make_async_copy(updated.at[slot], every.at[SLOTS * place.own + slot], local_sem.at[4 + slot]).wait()

    def place_unit(unit, carry):
        new_ref[unit] = every[slot_ref[unit]]
        return carry

    lax.fori_loop(0, 16, place_unit, 0)
    for slot in range(SLOTS):
        given(slot, 0)
        given(slot, 1)
        gathers[slot].finish()
    ring.finish()
    for copy in copies:
        copy.wait_send()


def precondition(slot_id, grads, left_rows, right_full, weights, adam):
    anywhere = pl.BlockSpec(memory_space=pl.ANY)
    vmem = pl.BlockSpec(memory_space=pltpu.VMEM)
    small = jax.ShapeDtypeStruct((SLOTS, ROWS, WIDTH), jnp.bfloat16)
    return pl.pallas_call(
        main_kernel,
        out_shape=(
            small,
            small,
            jax.ShapeDtypeStruct((16, ROWS, WIDTH), jnp.bfloat16),
            jax.ShapeDtypeStruct((SLOTS, WIDTH, WIDTH), jnp.bfloat16),
        ),
        in_specs=[pl.BlockSpec(memory_space=pltpu.SMEM), anywhere, vmem, anywhere, vmem, vmem],
        out_specs=(vmem, vmem, vmem, anywhere),
        scratch_shapes=[
            pltpu.VMEM((SLOTS, WIDTH, WIDTH), jnp.bfloat16),
            pltpu.VMEM((SLOTS, WIDTH, WIDTH), jnp.bfloat16),
            pltpu.VMEM((SLOTS, 3, ROWS, WIDTH), jnp.bfloat16),
            block_buffer(SLOTS),
            block_buffer(SLOTS),
            block_buffer(16 * SLOTS),
            pltpu.VMEM((8, 128), jnp.float32),
            pltpu.VMEM((15, 8, 128), jnp.float32),
            pltpu.SemaphoreType.DMA((SLOTS,)),
            pltpu.SemaphoreType.DMA((SLOTS,)),
            pltpu.SemaphoreType.DMA((3 * SLOTS,)),
            pltpu.SemaphoreType.DMA((3 * SLOTS,)),
            pltpu.SemaphoreType.DMA((1 + 2 * SLOTS,)),
            pltpu.SemaphoreType.DMA((15,)),
            pltpu.SemaphoreType.DMA((15,)),
            *RING_SEMS,
            *[pltpu.SemaphoreType.DMA((SLOTS, 8))] * 4,
        ],
        compiler_params=pltpu.CompilerParams(
            collective_id=1, has_side_effects=True, vmem_limit_bytes=60 * 1024 * 1024
        ),
        name="precondition",
    )(slot_id, grads, left_rows, right_full, weights, adam)


def slot_tables(owner_list, owner_count, slot_count, unit_count):
    index = jnp.arange(unit_count, dtype=jnp.int32)
    earlier = (owner_list[:, None] == owner_list[None, :]) & (index[None, :] < index[:, None])
    rank = jnp.sum(earlier.astype(jnp.int32), axis=1)
    slot_id = owner_list * slot_count + rank
    every_slot = jnp.arange(owner_count * slot_count, dtype=jnp.int32)
    match = (slot_id[None, :] == every_slot[:, None]).astype(jnp.int32)
    unit_of_slot = jnp.sum(match * index[None, :], axis=1)
    filled = jnp.sum(match, axis=1) > 0
    return (slot_id, unit_of_slot, filled)


def local(
    grad_parts, owner_list, left_stat, right_stat, second_moment, left_root, right_root, weights
):
    owner_count = lax.axis_size("own")
    unit_count = owner_list.shape[0]
    slot_id, unit_of_slot, filled = slot_tables(owner_list, owner_count, SLOTS, unit_count)
    me = lax.axis_index("own")
    units = lax.dynamic_slice_in_dim(unit_of_slot, me * SLOTS, SLOTS)
    mine = lax.dynamic_slice_in_dim(filled, me * SLOTS, SLOTS)

    parts = grad_parts.reshape(8, 2, ROWS, WIDTH)
    left_rows, right_full, summed = gather_roots(parts, left_root[0], right_root[0])
    grads = jnp.where(mine[:, None, None], jnp.take(summed, units, axis=0), jnp.bfloat16(0.0))

    gradient = grads.astype(jnp.float32)
    new_second = 0.95 * second_moment[0] + 0.05 * gradient * gradient
    adam = gradient / (jnp.sqrt(new_second) + 1e-08)
    adam_sums = jnp.sum(adam * adam, axis=(1, 2))
    adam_tile = jnp.broadcast_to(jnp.pad(adam_sums, (3, 2))[:, None], (8, 128))

    gram_left, gram_right, new_weights, _ = precondition(slot_id, grads, left_rows, right_full, weights[0], adam_tile)
    scale = 0.05 / WIDTH
    new_left = 0.95 * left_stat + scale * gram_left.astype(jnp.float32)[None]
    new_right = 0.95 * right_stat + scale * gram_right.astype(jnp.float32)[None]
    return (new_left, new_right, new_second[None], new_weights)


def solution(mesh):
    placed = P("own", None, "dp", None)
    in_specs = (placed, P(), placed, placed, placed, placed, placed, placed)
    out_specs = (placed, placed, placed, P(None, "dp", None))
    return jax.shard_map(local, mesh=mesh, in_specs=in_specs, out_specs=out_specs, check_vma=False)
```
